32 devices in a mesh: groups: 2 (over y), wide: 4 (over z), narrow: 4 (over x, core).
Axes of the slice: x: 2, y: 2, z: 4, core: 2. Of those that a mesh axis runs over, the one named last changes fastest.
Arguments:
- target_states: bfloat16 [256, 8192], P(('groups', 'wide'), 'narrow'), parts along dimension 0, may hold values from -6 to 6
- source_states: bfloat16 [256, 8192], P(('groups', 'wide'), 'narrow'), parts along dimension 0, may hold values from -6 to 6
- target_gate: bfloat16 [8192, 14336], P('narrow', 'wide'), may hold values from -0.0625 to 0.0625
- target_up: bfloat16 [8192, 14336], P('narrow', 'wide'), may hold values from -0.0625 to 0.0625
- source_gate: bfloat16 [8192, 14336], P('narrow', 'wide'), may hold values from -0.0625 to 0.0625
- source_up: bfloat16 [8192, 14336], P('narrow', 'wide'), may hold values from -0.0625 to 0.0625
- token_ids: int32 [256], P(('groups', 'narrow')), parts along dimension 0, may hold values from 0 to 128255
- lengths: int32 [16], P(('groups', 'narrow')), parts along dimension 0, may hold values from 1 to 16
- ratio_weight: float32 [128256], replicated, may hold values from 0.25 to 1
Outputs:
- target_hidden: bfloat16 [256, 14336], P(('groups', 'narrow'), 'wide'), parts along dimension 0
- ratio_hidden: bfloat16 [256, 14336], P(('groups', 'narrow'), 'wide'), parts along dimension 0
The draws below stay inside these ranges and needn't reach their ends.
There are 2 independent parts, one for each index of `groups`. The reference program is written for one: setup_inputs(seed, part) draws one part's arguments, and reference() takes and returns one part's arrays. A program takes and returns all parts, laid end to end along the dimension named above; an argument that names none is the same for every part. Nothing has to cross between parts.
All inputs are finite; a program needn't handle non-finite values.
Results may differ from the reference program's by a relative error of at most 0.02.
Values may be sent and summed in bfloat16 or wider, within the bound.
A program may use at most 128 MiB of HBM per device.

```python
import math
import jax
import jax.numpy as jnp
import numpy as np
from jax import lax

D = 8192
FF = 14336
VOCAB = 128256
HLEN = 16
TOKENS = 128
HYPS = 8
N_NARROW = 4


def with_ends(entries, key, smallest, high):
    longest = entries.shape.index(max(entries.shape))
    spots = []
    for shift in (0, 1):
        where = [jax.random.randint(jax.random.fold_in(key, axis), (), 0, length) for axis, length in enumerate(entries.shape)]
        where[longest] = (where[longest] + shift) % entries.shape[longest]
        spots.append(tuple(where))
    return entries.at[spots[0]].set(smallest).at[spots[1]].set(high)


def block_levels(key, extent, cuts, smallest, high):
    loudness = 1.0
    for dim, parts in cuts:
        heights = jax.random.uniform(jax.random.fold_in(jax.random.fold_in(key, 6), dim), (parts,), jnp.float32, smallest / len(cuts), high / len(cuts))
        loudness = loudness * jnp.repeat(jnp.exp(heights), extent[dim] // parts).reshape((-1,) + (1,) * (len(extent) - 1 - dim))
    return loudness


def skewed_wide(own_key, extent, number_of, slope):
    loads = [min(1 << octave, number_of + 1 - (1 << octave)) * (1 << 20) // math.isqrt((1 << octave) ** slope) + 1 for octave in range((number_of + 1).bit_length()) if 1 << octave <= number_of]
    spread = 1 + sum(loads) // (1 << 30)
    listing = np.cumsum(np.array([max(1, weight // spread) for weight in loads]))
    ticket = jax.random.randint(jax.random.fold_in(own_key, 1), extent, 0, int(listing[len(loads) - 1]))
    start = jnp.left_shift(1, jnp.searchsorted(jnp.asarray(listing, jnp.int32), ticket, side="right").astype(jnp.int32))
    standing = start - 1 + jax.random.randint(jax.random.fold_in(own_key, 4), extent, 0, 1 << 30) % jnp.minimum(start, number_of + 1 - start)
    return jax.random.permutation(jax.random.fold_in(own_key, 2), number_of)[standing].astype(jnp.int32)


def scatter_about(rng, shape, deviation, reach, shards=(), held_as=jnp.bfloat16):
    array = jax.random.normal(rng, shape, jnp.float32) * deviation
    if len(shards) > 0:
        array = block_levels(rng, shape, shards, -0.22, 0.18) * array
    return jnp.clip(array, min=-reach, max=reach).astype(held_as)


def setup_inputs(seed: int = 0, part: int = 0) -> dict:
    arg_keys = jax.random.split(jax.random.key(seed), 10)
    own_keys = jax.random.split(jax.random.fold_in(arg_keys[9], part), 10)
    target_states = scatter_about(own_keys[0], (TOKENS, D), 1.0, 6.0, ((0, 4), (1, 4)))
    source_states = scatter_about(own_keys[1], (TOKENS, D), 1.0, 6.0, ((0, 4), (1, 4)))
    target_gate = scatter_about(arg_keys[2], (D, FF), D ** -0.5, 0.0625, ((0, 4), (1, 4)))
    target_up = scatter_about(arg_keys[3], (D, FF), D ** -0.5, 0.0625, ((0, 4), (1, 4)))
    source_gate = scatter_about(arg_keys[4], (D, FF), D ** -0.5, 0.0625, ((0, 4), (1, 4)))
    source_up = scatter_about(arg_keys[5], (D, FF), D ** -0.5, 0.0625, ((0, 4), (1, 4)))
    token_ids = with_ends(skewed_wide(own_keys[6], (TOKENS,), VOCAB, 2), jax.random.fold_in(own_keys[6], 3), 0, VOCAB - 1).astype(jnp.int32)
    lengths = with_ends(jax.random.randint(own_keys[7], (HYPS,), 1, HLEN + 1), jax.random.fold_in(own_keys[7], 1), 1, HLEN).astype(jnp.int32)
    ratio_weight = jnp.clip(jnp.exp(jax.random.uniform(arg_keys[8], (VOCAB,), jnp.float32, math.log(0.25), math.log(1.0))), 0.25, 1.0)
    return dict(target_states=target_states, source_states=source_states, target_gate=target_gate, target_up=target_up, source_gate=source_gate, source_up=source_up, token_ids=token_ids, lengths=lengths, ratio_weight=ratio_weight)


def projected(states, weight):
    tile = D // N_NARROW
    total = jnp.zeros((states.shape[0], weight.shape[1]), jnp.float32)
    for index in range(N_NARROW):
        partial_sum = jnp.dot(states[:, index * tile:(index + 1) * tile], weight[index * tile:(index + 1) * tile, :], preferred_element_type=jnp.float32)
        rounded = lax.optimization_barrier(partial_sum.astype(jnp.bfloat16))
        total = total + rounded.astype(jnp.float32)
    return total


def reference(target_states, source_states, target_gate, target_up, source_gate, source_up, token_ids, lengths, ratio_weight):
    target_act = jax.nn.silu(projected(target_states, target_gate)) * projected(target_states, target_up)
    source_act = jax.nn.silu(projected(source_states, source_gate)) * projected(source_states, source_up)
    slots = jnp.arange(HLEN, dtype=jnp.int32)
    live = (slots[None, :] < lengths[:, None]).reshape(-1).astype(jnp.float32)
    weight = ratio_weight[token_ids]
    target_out = (live[:, None] * target_act).astype(jnp.bfloat16)
    ratio_out = (live[:, None] * (target_act - weight[:, None] * source_act)).astype(jnp.bfloat16)
    return target_out, ratio_out
```

```python
import functools

import jax
import jax.numpy as jnp
from jax import lax
from jax.experimental import pallas as pl
from jax.experimental.pallas import tpu as pltpu
from jax.sharding import PartitionSpec as P

MESH = pl.DeviceIdType.MESH
VMEM_BYTES = 67_000_000


def matmul(left, right):
    return jnp.dot(left, right, preferred_element_type=jnp.float32)


def pair_project(w_gate, w_upper, piece):
    return jnp.concatenate([matmul(piece, w_gate), matmul(piece, w_upper)], axis=1)


def gated(summed, hidden_cols):
    return jax.nn.silu(summed[:, :hidden_cols]) * summed[:, hidden_cols:]


def kernel(
    wide, tn, slots,
    live_ref, weight_ref, ts_ref, ss_ref, tg_ref, tu_ref, sg_ref, su_ref,
    t_out, r_out,
    gath, wbuf, part, a_send, a_recv, b_send, b_recv, kept,
    own_sem, g_send, g_recv, w_sem, as_sem, ar_sem, bs_sem, br_sem,
):
    w = lax.axis_index("wide")
    n = lax.axis_index("narrow")
    x = n // 2
    c = n % 2
    mate = 2 * x + (1 - c)
    across = 2 * (1 - x) + c
    cols = tg_ref.shape[1]
    per = cols // tn
    units = 2 * per
    rows = part.shape[3]

    def weight_copies(u, slot, model, j):
        pair = (tg_ref, tu_ref) if model == 0 else (sg_ref, su_ref)
        span = pl.ds(pl.multiple_of(j * tn, tn), tn)
        return [
            pltpu.make_async_copy(pair[k].at[:, span], wbuf.at[slot, k], w_sem.at[slot, k])
            for k in range(2)
        ]

    def load(u):
        slot = u % slots

        @pl.when(u < per)
        def _():
            for copy in weight_copies(u, slot, 0, u):
                copy.start()

        @pl.when(jnp.logical_and(u >= per, u < units))
        def _():
            for copy in weight_copies(u, slot, 1, u - per):
                copy.start()

    own = [
        pltpu.make_async_copy(ref, gath.at[m, w], own_sem.at[m])
        for m, ref in enumerate((ts_ref, ss_ref))
    ]
    for copy in own:
        copy.start()
    for u in range(min(slots, units)):
        for copy in weight_copies(u, u, u // per, u % per):
            copy.start()

    barrier = pltpu.get_barrier_semaphore()

    def greet(axis, index):
        pl.semaphore_signal(barrier, inc=1, device_id={axis: index}, device_id_type=MESH)

    greet("narrow", mate)
    greet("narrow", across)

    @pl.when(w > 0)
    def _():
        greet("wide", w - 1)

    @pl.when(w < wide - 1)
    def _():
        greet("wide", w + 1)

    inner = jnp.logical_and(w > 0, w < wide - 1)
    pl.semaphore_wait(barrier, jnp.where(inner, 4, 3))

    def hop(m, block, up):
        return pltpu.make_async_remote_copy(
            src_ref=gath.at[m, block],
            dst_ref=gath.at[m, block],
            send_sem=g_send.at[m, 0 if up else 1, block],
            recv_sem=g_recv.at[m, block],
            device_id={"wide": w + 1 if up else w - 1},
            device_id_type=MESH,
        )

    def gather_step(m, s):
        @pl.when(w - s >= 0)
        def _():
            if s > 0:
                hop(m, w - s, True).wait_recv()

            @pl.when(w < wide - 1)
            def _():
                hop(m, w - s, True).start()

        @pl.when(w + s <= wide - 1)
        def _():
            if s > 0:
                hop(m, w + s, False).wait_recv()

            @pl.when(w > 0)
            def _():
                hop(m, w + s, False).start()

        if m == 0:
            @pl.when(jnp.logical_and(w == s, w < wide - 1))
            def _():
                hop(1, w, True).start()

            @pl.when(jnp.logical_and(wide - 1 - w == s, w > 0))
            def _():
                hop(1, w, False).start()

    for copy in own:
        copy.wait()
    for s in range(wide):
        gather_step(0, s)

    def a_copy(u):
        return pltpu.make_async_remote_copy(
            src_ref=a_send.at[u], dst_ref=a_recv.at[u],
            send_sem=as_sem.at[u], recv_sem=ar_sem.at[u],
            device_id={"narrow": mate}, device_id_type=MESH,
        )

    def b_copy(u):
        return pltpu.make_async_remote_copy(
            src_ref=b_send.at[u], dst_ref=b_recv.at[u],
            send_sem=bs_sem.at[u], recv_sem=br_sem.at[u],
            device_id={"narrow": across}, device_id_type=MESH,
        )

    def cross(u):
        a_copy(u).wait_recv()
        for k in range(2):
            total = part[u, k, across] + a_recv[u, 1 - x, k].astype(jnp.float32)
            b_send[u, k] = total.astype(jnp.bfloat16)
        b_copy(u).start()

    def unit(u, carry):
        for s in range(1, wide):
            @pl.when(u == min(1 + 2 * s, per))
            def _():
                gather_step(1, s)

        slot = u % slots
        model = u // per
        left = gath[model].reshape(4 * rows, gath.shape[3])
        for k in range(2):
            weight_copies(u, slot, 0, 0)[k].wait()
            part[u, k] = matmul(left, wbuf[slot, k]).reshape(4, rows, tn)
        load(u + slots)
        for i in range(2):
            for k in range(2):
                a_send[u, i, k] = part[u, k, 2 * i + 1 - c].astype(jnp.bfloat16)
        a_copy(u).start()

        @pl.when(u > 0)
        def _():
            cross(u - 1)

        return carry

    lax.fori_loop(0, units, unit, 0)
    cross(units - 1)

    def summed(u, k):
        near = part[u, k, n] + a_recv[u, x, k].astype(jnp.float32)
        return near + b_recv[u, k].astype(jnp.float32)

    def activation(u):
        b_copy(u).wait_recv()
        gate = summed(u, 0)
        return gate / (1.0 + jnp.exp(-gate)) * summed(u, 1)

    def finish_target(j, carry):
        act = activation(j)
        kept[j] = act
        t_out[:, pl.ds(pl.multiple_of(j * tn, tn), tn)] = (live_ref[...] * act).astype(t_out.dtype)
        return carry

    def finish_ratio(j, carry):
        act = activation(per + j)
        ratio = live_ref[...] * (kept[j] - weight_ref[...] * act)
        r_out[:, pl.ds(pl.multiple_of(j * tn, tn), tn)] = ratio.astype(r_out.dtype)
        return carry

    lax.fori_loop(0, per, finish_target, 0)
    lax.fori_loop(0, per, finish_ratio, 0)

    def drain(u, carry):
        a_copy(u).wait_send()
        b_copy(u).wait_send()
        return carry

    lax.fori_loop(0, units, drain, 0)
    for m in range(2):
        for block in range(wide):
            @pl.when(jnp.logical_and(block <= w, w < wide - 1))
            def _():
                hop(m, block, True).wait_send()

            @pl.when(jnp.logical_and(block >= w, w > 0))
            def _():
                hop(m, block, False).wait_send()


def plan(states, weights, wide, narrow):
    cols = weights.shape[1]
    tokens = states.shape[0] * wide
    if narrow != 4 or wide < 2 or tokens % 64 or states.shape[0] % 16:
        return None
    for tn in (512, 256):
        if cols % tn:
            continue
        units = 2 * cols // tn
        unit_bytes = tn * tokens * 2 * (4 + 1 + 1 + 1)
        fixed = 2 * tokens * states.shape[1] * 2 + cols * tokens * 4 + units * unit_bytes
        slots = (VMEM_BYTES - 8_000_000 - fixed) // (4 * tn * states.shape[1])
        slots = min(slots, units)
        if slots >= 2:
            return tn, slots
    return None


def fused(states, weights, live, weight, wide, tn, slots):
    rows = states[0].shape[0] * wide // 4
    depth = states[0].shape[1]
    cols = weights[0].shape[1]
    units = 2 * cols // tn
    vmem = pl.BlockSpec(memory_space=pltpu.VMEM)
    hbm = pl.BlockSpec(memory_space=pl.ANY)
    out = jax.ShapeDtypeStruct((rows, cols), jnp.bfloat16)
    dma = pltpu.SemaphoreType.DMA
    return pl.pallas_call(
        functools.partial(kernel, wide, tn, slots),
        out_shape=(out, out),
        in_specs=[vmem, vmem] + [hbm] * 6,
        out_specs=(vmem, vmem),
        scratch_shapes=[
            pltpu.VMEM((2, wide, states[0].shape[0], depth), jnp.bfloat16),
            pltpu.VMEM((slots, 2, depth, tn), jnp.bfloat16),
            pltpu.VMEM((units, 2, 4, rows, tn), jnp.float32),
            pltpu.VMEM((units, 2, 2, rows, tn), jnp.bfloat16),
            pltpu.VMEM((units, 2, 2, rows, tn), jnp.bfloat16),
            pltpu.VMEM((units, 2, rows, tn), jnp.bfloat16),
            pltpu.VMEM((units, 2, rows, tn), jnp.bfloat16),
            pltpu.VMEM((units // 2, rows, tn), jnp.float32),
            dma((2,)),
            dma((2, 2, wide)),
            dma((2, wide)),
            dma((slots, 2)),
            dma((units,)),
            dma((units,)),
            dma((units,)),
            dma((units,)),
        ],
        compiler_params=pltpu.CompilerParams(
            collective_id=0, has_side_effects=True, vmem_limit_bytes=VMEM_BYTES
        ),
        name="rescore",
    )(live, weight, *states, *weights)


def local(
    wide,
    narrow,
    target_states,
    source_states,
    target_gate,
    target_up,
    source_gate,
    source_up,
    token_ids,
    lengths,
    ratio_weight,
):
    hidden_cols = target_gate.shape[1]
    own_rows = token_ids.shape[0]
    slot_count = own_rows // lengths.shape[0]
    slots = jnp.arange(slot_count, dtype=jnp.int32)
    live = (slots[None, :] < lengths[:, None]).reshape(-1).astype(jnp.float32)
    weight = ratio_weight[token_ids]
    chosen = plan(target_states, target_gate, wide, narrow)
    if chosen is not None:
        return fused(
            (target_states, source_states),
            (target_gate, target_up, source_gate, source_up),
            live[:, None],
            weight[:, None],
            wide,
            *chosen,
        )
    target_terms = pair_project(
        target_gate, target_up, lax.all_gather(target_states, "wide", axis=0, tiled=True)
    )
    source_terms = pair_project(
        source_gate, source_up, lax.all_gather(source_states, "wide", axis=0, tiled=True)
    )
    target_sum, source_sum = (
        lax.psum_scatter(
            target_terms.astype(jnp.bfloat16), "narrow", scatter_dimension=0, tiled=True
        ).astype(jnp.float32),
        lax.psum_scatter(
            source_terms.astype(jnp.bfloat16), "narrow", scatter_dimension=0, tiled=True
        ).astype(jnp.float32),
    )
    target_act = gated(target_sum, hidden_cols)
    source_act = gated(source_sum, hidden_cols)
    target_out = (live[:, None] * target_act).astype(jnp.bfloat16)
    ratio_out = (live[:, None] * (target_act - weight[:, None] * source_act)).astype(jnp.bfloat16)
    return (target_out, ratio_out)


def solution(mesh):
    placed = (
        P(("groups", "wide"), "narrow"),
        P(("groups", "wide"), "narrow"),
        P("narrow", "wide"),
        P("narrow", "wide"),
        P("narrow", "wide"),
        P("narrow", "wide"),
        P(("groups", "narrow")),
        P(("groups", "narrow")),
        P(),
    )
    return jax.shard_map(
        functools.partial(local, mesh.shape["wide"], mesh.shape["narrow"]),
        mesh=mesh,
        in_specs=placed,
        out_specs=(P(("groups", "narrow"), "wide"), P(("groups", "narrow"), "wide")),
        check_vma=False,
    )
```

```python
import functools

import jax
import jax.numpy as jnp
from jax import lax
from jax.experimental import pallas as pl
from jax.experimental.pallas import tpu as pltpu
from jax.sharding import PartitionSpec as P

MESH = pl.DeviceIdType.MESH
VMEM_BYTES = 67_000_000


def matmul(left, right):
    return jnp.dot(left, right, preferred_element_type=jnp.float32)


def pair_project(w_gate, w_upper, piece):
    return jnp.concatenate([matmul(piece, w_gate), matmul(piece, w_upper)], axis=1)


def gated(summed, hidden_cols):
    return jax.nn.silu(summed[:, :hidden_cols]) * summed[:, hidden_cols:]


def kernel(
    wide, tn, slots,
    ids_ref, len_ref, table_ref, ts_ref, ss_ref, tg_ref, tu_ref, sg_ref, su_ref,
    t_out, r_out,
    gath, wbuf, part, a_send, a_recv, b_send, b_recv, kept,
    live_ref, weight_ref, table, table_sem, own_sem, g_send, g_recv, w_sem, as_sem, ar_sem, bs_sem, br_sem,
):
    w = lax.axis_index("wide")
    n = lax.axis_index("narrow")
    x = n // 2
    c = n % 2
    mate = 2 * x + (1 - c)
    across = 2 * (1 - x) + c
    cols = tg_ref.shape[1]
    per = cols // tn
    units = 2 * per
    rows = part.shape[3]

    def weight_copies(slot, model, j):
        pair = (tg_ref, tu_ref) if model == 0 else (sg_ref, su_ref)
        span = pl.ds(pl.multiple_of(j * tn, tn), tn)
        return [
            pltpu.make_async_copy(pair[k].at[:, span], wbuf.at[slot, k], w_sem.at[slot, k])
            for k in range(2)
        ]

    def load(u):
        slot = u % slots

        @pl.when(u < per)
        def _():
            for copy in weight_copies(slot, 0, u):
                copy.start()

        @pl.when(jnp.logical_and(u >= per, u < units))
        def _():
            for copy in weight_copies(slot, 1, u - per):
                copy.start()

    own = [
        pltpu.make_async_copy(ref, gath.at[m, w], own_sem.at[m])
        for m, ref in enumerate((ts_ref, ss_ref))
    ]
    for copy in own:
        copy.start()

    def load_ahead(first, last):
        for u in range(first, min(last, slots, units)):
            for copy in weight_copies(u, u // per, u % per):
                copy.start()

    load_ahead(0, 1)
    fetch = pltpu.make_async_copy(table_ref, table, table_sem)
    fetch.start()
    barrier = pltpu.get_barrier_semaphore()

    def greet(axis, index):
        pl.semaphore_signal(barrier, inc=1, device_id={axis: index}, device_id_type=MESH)

    greet("narrow", mate)
    greet("narrow", across)

    @pl.when(w > 0)
    def _():
        greet("wide", w - 1)

    @pl.when(w < wide - 1)
    def _():
        greet("wide", w + 1)

    inner = jnp.logical_and(w > 0, w < wide - 1)
    pl.semaphore_wait(barrier, jnp.where(inner, 4, 3))

    def hop(m, block, up):
        return pltpu.make_async_remote_copy(
            src_ref=gath.at[m, block],
            dst_ref=gath.at[m, block],
            send_sem=g_send.at[m, 0 if up else 1, block],
            recv_sem=g_recv.at[m, block],
            device_id={"wide": w + 1 if up else w - 1},
            device_id_type=MESH,
        )

    def gather_step(m, s):
        @pl.when(w - s >= 0)
        def _():
            if s > 0:
                hop(m, w - s, True).wait_recv()

            @pl.when(w < wide - 1)
            def _():
                hop(m, w - s, True).start()

        @pl.when(w + s <= wide - 1)
        def _():
            if s > 0:
                hop(m, w + s, False).wait_recv()

            @pl.when(w > 0)
            def _():
                hop(m, w + s, False).start()

        if m == 0:
            @pl.when(jnp.logical_and(w == s, w < wide - 1))
            def _():
                hop(1, w, True).start()

            @pl.when(jnp.logical_and(wide - 1 - w == s, w > 0))
            def _():
                hop(1, w, False).start()

    for copy in own:
        copy.wait()
    batch = pl.cdiv(slots - 1, wide)
    for s in range(wide):
        gather_step(0, s)
        load_ahead(1 + s * batch, 1 + (s + 1) * batch)

    def a_copy(u):
        return pltpu.make_async_remote_copy(
            src_ref=a_send.at[u], dst_ref=a_recv.at[u],
            send_sem=as_sem.at[u], recv_sem=ar_sem.at[u],
            device_id={"narrow": mate}, device_id_type=MESH,
        )

    def b_copy(u):
        return pltpu.make_async_remote_copy(
            src_ref=b_send.at[u], dst_ref=b_recv.at[u],
            send_sem=bs_sem.at[u], recv_sem=br_sem.at[u],
            device_id={"narrow": across}, device_id_type=MESH,
        )

    def cross(u):
        a_copy(u).wait_recv()
        for k in range(2):
            total = part[u, k, across] + a_recv[u, 1 - x, k].astype(jnp.float32)
            b_send[u, k] = total.astype(jnp.bfloat16)
        b_copy(u).start()

    def unit(u, carry):
        for s in range(1, wide):
            @pl.when(u == min(1 + 2 * s, per))
            def _():
                gather_step(1, s)

        slot = u % slots
        model = u // per
        left = gath[model].reshape(4 * rows, gath.shape[3])
        for k in range(2):
            weight_copies(slot, 0, 0)[k].wait()
            part[u, k] = matmul(left, wbuf[slot, k]).reshape(4, rows, tn)
        for i in range(2):
            for k in range(2):
                a_send[u, i, k] = part[u, k, 2 * i + 1 - c].astype(jnp.bfloat16)
        a_copy(u).start()

        @pl.when(u > 0)
        def _():
            cross(u - 1)

        load(u + slots)
        return carry

    lax.fori_loop(0, units, unit, 0)
    cross(units - 1)

    fetch.wait()
    row = lax.broadcasted_iota(jnp.int32, (rows, 1), 0)
    hlen = rows // len_ref.shape[0]
    lived = jnp.zeros((rows, 1), jnp.float32)
    for h in range(len_ref.shape[0]):
        inside = jnp.logical_and(row >= h * hlen, row < h * hlen + len_ref[h])
        lived = jnp.where(inside, 1.0, lived)
    weights = jnp.zeros((rows, 1), jnp.float32)
    for i in range(rows):
        weights = jnp.where(row == i, table[ids_ref[i]], weights)
    live_ref[...] = lived
    weight_ref[...] = weights

    def summed(u, k):
        near = part[u, k, n] + a_recv[u, x, k].astype(jnp.float32)
        return near + b_recv[u, k].astype(jnp.float32)

    def activation(u):
        b_copy(u).wait_recv()
        gate = summed(u, 0)
        return gate / (1.0 + jnp.exp(-gate)) * summed(u, 1)

    def finish_target(j, carry):
        act = activation(j)
        kept[j] = act
        t_out[:, pl.ds(pl.multiple_of(j * tn, tn), tn)] = (live_ref[...] * act).astype(t_out.dtype)
        return carry

    def finish_ratio(j, carry):
        act = activation(per + j)
        ratio = live_ref[...] * (kept[j] - weight_ref[...] * act)
        r_out[:, pl.ds(pl.multiple_of(j * tn, tn), tn)] = ratio.astype(r_out.dtype)
        return carry

    lax.fori_loop(0, per, finish_target, 0)
    lax.fori_loop(0, per, finish_ratio, 0)

    def drain(u, carry):
        a_copy(u).wait_send()
        b_copy(u).wait_send()
        return carry

    lax.fori_loop(0, units, drain, 0)
    for m in range(2):
        for block in range(wide):
            @pl.when(jnp.logical_and(block <= w, w < wide - 1))
            def _():
                hop(m, block, True).wait_send()

            @pl.when(jnp.logical_and(block >= w, w > 0))
            def _():
                hop(m, block, False).wait_send()


def hand_over(*refs):
    taken, given, held, in_sem, out_sem = refs[:2], refs[2:4], refs[4], refs[5], refs[6]
    arrive = [pltpu.make_async_copy(taken[i], held.at[i], in_sem.at[i]) for i in range(2)]
    leave = [pltpu.make_async_copy(held.at[i], given[i], out_sem.at[i]) for i in range(2)]
    for copy in arrive:
        copy.start()
    for i in range(2):
        arrive[i].wait()
        leave[i].start()
    for copy in leave:
        copy.wait()


def plan(states, weights, wide, narrow):
    cols = weights.shape[1]
    tokens = states.shape[0] * wide
    if narrow != 4 or wide < 2 or tokens % 64 or states.shape[0] % 16:
        return None
    for tn in (512, 256):
        if cols % tn:
            continue
        units = 2 * cols // tn
        unit_bytes = tn * tokens * 2 * (4 + 1 + 1 + 1)
        fixed = 2 * tokens * states.shape[1] * 2 + cols * tokens * 4 + units * unit_bytes
        slots = (VMEM_BYTES - 8_000_000 - fixed) // (4 * tn * states.shape[1])
        slots = min(slots, units)
        if slots >= 2:
            return tn, slots
    return None


def fused(states, weights, token_ids, lengths, ratio_weight, wide, tn, slots):
    rows = states[0].shape[0] * wide // 4
    depth = states[0].shape[1]
    cols = weights[0].shape[1]
    units = 2 * cols // tn
    smem = pl.BlockSpec(memory_space=pltpu.SMEM)
    vmem = pl.BlockSpec(memory_space=pltpu.VMEM)
    hbm = pl.BlockSpec(memory_space=pl.ANY)
    out = jax.ShapeDtypeStruct((rows, cols), jnp.bfloat16)
    dma = pltpu.SemaphoreType.DMA
    pair = pl.pallas_call(
        functools.partial(kernel, wide, tn, slots),
        out_shape=(out, out),
        in_specs=[smem, smem] + [hbm] * 7,
        out_specs=(vmem, vmem),
        scratch_shapes=[
            pltpu.VMEM((2, wide, states[0].shape[0], depth), jnp.bfloat16),
            pltpu.VMEM((slots, 2, depth, tn), jnp.bfloat16),
            pltpu.VMEM((units, 2, 4, rows, tn), jnp.float32),
            pltpu.VMEM((units, 2, 2, rows, tn), jnp.bfloat16),
            pltpu.VMEM((units, 2, 2, rows, tn), jnp.bfloat16),
            pltpu.VMEM((units, 2, rows, tn), jnp.bfloat16),
            pltpu.VMEM((units, 2, rows, tn), jnp.bfloat16),
            pltpu.VMEM((units // 2, rows, tn), jnp.float32),
            pltpu.VMEM((rows, 1), jnp.float32),
            pltpu.VMEM((rows, 1), jnp.float32),
            pltpu.SMEM(ratio_weight.shape, jnp.float32),
            dma,
            dma((2,)),
            dma((2, 2, wide)),
            dma((2, wide)),
            dma((slots, 2)),
            dma((units,)),
            dma((units,)),
            dma((units,)),
            dma((units,)),
        ],
        compiler_params=pltpu.CompilerParams(
            collective_id=0, has_side_effects=True, vmem_limit_bytes=VMEM_BYTES
        ),
        name="rescore",
    )(token_ids, lengths, ratio_weight, *states, *weights)
    return pl.pallas_call(
        hand_over,
        out_shape=(out, out),
        in_specs=[hbm, hbm],
        out_specs=(hbm, hbm),
        scratch_shapes=[pltpu.VMEM((2, rows, cols), jnp.bfloat16), dma((2,)), dma((2,))],
        name="hand_over",
    )(*pair)


def local(
    wide,
    narrow,
    target_states,
    source_states,
    target_gate,
    target_up,
    source_gate,
    source_up,
    token_ids,
    lengths,
    ratio_weight,
):
    hidden_cols = target_gate.shape[1]
    own_rows = token_ids.shape[0]
    chosen = plan(target_states, target_gate, wide, narrow)
    if chosen is not None:
        return fused(
            (target_states, source_states),
            (target_gate, target_up, source_gate, source_up),
            token_ids,
            lengths,
            ratio_weight,
            wide,
            *chosen,
        )
    slot_count = own_rows // lengths.shape[0]
    slots = jnp.arange(slot_count, dtype=jnp.int32)
    live = (slots[None, :] < lengths[:, None]).reshape(-1).astype(jnp.float32)
    weight = ratio_weight[token_ids]
    target_terms = pair_project(
        target_gate, target_up, lax.all_gather(target_states, "wide", axis=0, tiled=True)
    )
    source_terms = pair_project(
        source_gate, source_up, lax.all_gather(source_states, "wide", axis=0, tiled=True)
    )
    target_sum, source_sum = (
        lax.psum_scatter(
            target_terms.astype(jnp.bfloat16), "narrow", scatter_dimension=0, tiled=True
        ).astype(jnp.float32),
        lax.psum_scatter(
            source_terms.astype(jnp.bfloat16), "narrow", scatter_dimension=0, tiled=True
        ).astype(jnp.float32),
    )
    target_act = gated(target_sum, hidden_cols)
    source_act = gated(source_sum, hidden_cols)
    target_out = (live[:, None] * target_act).astype(jnp.bfloat16)
    ratio_out = (live[:, None] * (target_act - weight[:, None] * source_act)).astype(jnp.bfloat16)
    return (target_out, ratio_out)


def solution(mesh):
    placed = (
        P(("groups", "wide"), "narrow"),
        P(("groups", "wide"), "narrow"),
        P("narrow", "wide"),
        P("narrow", "wide"),
        P("narrow", "wide"),
        P("narrow", "wide"),
        P(("groups", "narrow")),
        P(("groups", "narrow")),
        P(),
    )
    return jax.shard_map(
        functools.partial(local, mesh.shape["wide"], mesh.shape["narrow"]),
        mesh=mesh,
        in_specs=placed,
        out_specs=(P(("groups", "narrow"), "wide"), P(("groups", "narrow"), "wide")),
        check_vma=False,
    )
```

```python
import functools

import jax
import jax.numpy as jnp
from jax import lax
from jax.experimental import pallas as pl
from jax.experimental.pallas import tpu as pltpu
from jax.sharding import PartitionSpec as P

MESH = pl.DeviceIdType.MESH
VMEM_BYTES = 67_000_000


def matmul(left, right):
    return jnp.dot(left, right, preferred_element_type=jnp.float32)


def pair_project(w_gate, w_upper, piece):
    return jnp.concatenate([matmul(piece, w_gate), matmul(piece, w_upper)], axis=1)


def gated(summed, hidden_cols):
    return jax.nn.silu(summed[:, :hidden_cols]) * summed[:, hidden_cols:]


def kernel(
    wide, tn, slots,
    ids_ref, len_ref, table_ref, ts_ref, ss_ref, tg_ref, tu_ref, sg_ref, su_ref,
    t_out, r_out,
    gath, wbuf, part, a_send, a_recv, b_send, b_recv, kept,
    live_ref, weight_ref, table, table_sem, own_sem, g_send, g_recv, w_sem, as_sem, ar_sem, bs_sem, br_sem,
):
    w = lax.axis_index("wide")
    n = lax.axis_index("narrow")
    x = n // 2
    c = n % 2
    mate = 2 * x + (1 - c)
    across = 2 * (1 - x) + c
    cols = tg_ref.shape[1]
    per = cols // tn
    units = 2 * per
    rows = part.shape[3]

    def weight_copies(slot, model, j):
        pair = (tg_ref, tu_ref) if model == 0 else (sg_ref, su_ref)
        span = pl.ds(pl.multiple_of(j * tn, tn), tn)
        return [
            pltpu.make_async_copy(pair[k].at[:, span], wbuf.at[slot, k], w_sem.at[slot, k])
            for k in range(2)
        ]

    def load(u):
        slot = u % slots

        @pl.when(u < per)
        def _():
            for copy in weight_copies(slot, 0, u):
                copy.start()

        @pl.when(jnp.logical_and(u >= per, u < units))
        def _():
            for copy in weight_copies(slot, 1, u - per):
                copy.start()

    own = [
        pltpu.make_async_copy(ref, gath.at[m, w], own_sem.at[m])
        for m, ref in enumerate((ts_ref, ss_ref))
    ]
    for copy in own:
        copy.start()

    def load_ahead(first, last):
        for u in range(first, min(last, slots, units)):
            for copy in weight_copies(u, u // per, u % per):
                copy.start()

    load_ahead(0, 1)
    fetch = pltpu.make_async_copy(table_ref, table, table_sem)
    barrier = pltpu.get_barrier_semaphore()

    def greet(axis, index):
        pl.semaphore_signal(barrier, inc=1, device_id={axis: index}, device_id_type=MESH)

    greet("narrow", mate)
    greet("narrow", across)

    @pl.when(w > 0)
    def _():
        greet("wide", w - 1)

    @pl.when(w < wide - 1)
    def _():
        greet("wide", w + 1)

    inner = jnp.logical_and(w > 0, w < wide - 1)
    pl.semaphore_wait(barrier, jnp.where(inner, 4, 3))

    def hop(m, block, up):
        return pltpu.make_async_remote_copy(
            src_ref=gath.at[m, block],
            dst_ref=gath.at[m, block],
            send_sem=g_send.at[m, 0 if up else 1, block],
            recv_sem=g_recv.at[m, block],
            device_id={"wide": w + 1 if up else w - 1},
            device_id_type=MESH,
        )

    def gather_step(m, s):
        @pl.when(w - s >= 0)
        def _():
            if s > 0:
                hop(m, w - s, True).wait_recv()

            @pl.when(w < wide - 1)
            def _():
                hop(m, w - s, True).start()

        @pl.when(w + s <= wide - 1)
        def _():
            if s > 0:
                hop(m, w + s, False).wait_recv()

            @pl.when(w > 0)
            def _():
                hop(m, w + s, False).start()

        if m == 0:
            @pl.when(jnp.logical_and(w == s, w < wide - 1))
            def _():
                hop(1, w, True).start()

            @pl.when(jnp.logical_and(wide - 1 - w == s, w > 0))
            def _():
                hop(1, w, False).start()

    for copy in own:
        copy.wait()
    batch = pl.cdiv(slots - 1, wide)
    for s in range(wide):
        gather_step(0, s)
        load_ahead(1 + s * batch, 1 + (s + 1) * batch)
    fetch.start()

    def a_copy(u):
        return pltpu.make_async_remote_copy(
            src_ref=a_send.at[u], dst_ref=a_recv.at[u],
            send_sem=as_sem.at[u], recv_sem=ar_sem.at[u],
            device_id={"narrow": mate}, device_id_type=MESH,
        )

    def b_copy(u):
        return pltpu.make_async_remote_copy(
            src_ref=b_send.at[u], dst_ref=b_recv.at[u],
            send_sem=bs_sem.at[u], recv_sem=br_sem.at[u],
            device_id={"narrow": across}, device_id_type=MESH,
        )

    def cross(u):
        a_copy(u).wait_recv()
        for k in range(2):
            total = part[u, k, across] + a_recv[u, 1 - x, k].astype(jnp.float32)
            b_send[u, k] = total.astype(jnp.bfloat16)
        b_copy(u).start()

    def unit(u, carry):
        for s in range(1, wide):
            @pl.when(u == min(1 + 2 * s, per))
            def _():
                gather_step(1, s)

        slot = u % slots
        model = u // per
        left = gath[model].reshape(4 * rows, gath.shape[3])
        for k in range(2):
            weight_copies(slot, 0, 0)[k].wait()
            part[u, k] = matmul(left, wbuf[slot, k]).reshape(4, rows, tn)
        for i in range(2):
            for k in range(2):
                a_send[u, i, k] = part[u, k, 2 * i + 1 - c].astype(jnp.bfloat16)
        a_copy(u).start()

        @pl.when(u > 0)
        def _():
            cross(u - 1)

        load(u + slots)
        return carry

    lax.fori_loop(0, units, unit, 0)
    cross(units - 1)

    fetch.wait()
    row = lax.broadcasted_iota(jnp.int32, (rows, 1), 0)
    hlen = rows // len_ref.shape[0]
    lived = jnp.zeros((rows, 1), jnp.float32)
    for h in range(len_ref.shape[0]):
        inside = jnp.logical_and(row >= h * hlen, row < h * hlen + len_ref[h])
        lived = jnp.where(inside, 1.0, lived)
    weights = jnp.zeros((rows, 1), jnp.float32)
    for i in range(rows):
        weights = jnp.where(row == i, table[ids_ref[i]], weights)
    live_ref[...] = lived
    weight_ref[...] = weights

    def summed(u, k):
        near = part[u, k, n] + a_recv[u, x, k].astype(jnp.float32)
        return near + b_recv[u, k].astype(jnp.float32)

    def activation(u):
        b_copy(u).wait_recv()
        gate = summed(u, 0)
        return gate / (1.0 + jnp.exp(-gate)) * summed(u, 1)

    def finish_target(j, carry):
        act = activation(j)
        kept[j] = act
        t_out[:, pl.ds(pl.multiple_of(j * tn, tn), tn)] = (live_ref[...] * act).astype(t_out.dtype)
        return carry

    def finish_ratio(j, carry):
        act = activation(per + j)
        ratio = live_ref[...] * (kept[j] - weight_ref[...] * act)
        r_out[:, pl.ds(pl.multiple_of(j * tn, tn), tn)] = ratio.astype(r_out.dtype)
        return carry

    lax.fori_loop(0, per, finish_target, 0)
    lax.fori_loop(0, per, finish_ratio, 0)

    def drain(u, carry):
        a_copy(u).wait_send()
        b_copy(u).wait_send()
        return carry

    lax.fori_loop(0, units, drain, 0)
    for m in range(2):
        for block in range(wide):
            @pl.when(jnp.logical_and(block <= w, w < wide - 1))
            def _():
                hop(m, block, True).wait_send()

            @pl.when(jnp.logical_and(block >= w, w > 0))
            def _():
                hop(m, block, False).wait_send()


def hand_over(*refs):
    taken, given, held, in_sem, out_sem = refs[:2], refs[2:4], refs[4], refs[5], refs[6]
    arrive = [pltpu.make_async_copy(taken[i], held.at[i], in_sem.at[i]) for i in range(2)]
    leave = [pltpu.make_async_copy(held.at[i], given[i], out_sem.at[i]) for i in range(2)]
    for copy in arrive:
        copy.start()
    for i in range(2):
        arrive[i].wait()
        leave[i].start()
    for copy in leave:
        copy.wait()


def plan(states, weights, wide, narrow):
    cols = weights.shape[1]
    tokens = states.shape[0] * wide
    if narrow != 4 or wide < 2 or tokens % 64 or states.shape[0] % 16:
        return None
    for tn in (512, 256):
        if cols % tn:
            continue
        units = 2 * cols // tn
        unit_bytes = tn * tokens * 2 * (4 + 1 + 1 + 1)
        fixed = 2 * tokens * states.shape[1] * 2 + cols * tokens * 4 + units * unit_bytes
        slots = (VMEM_BYTES - 8_000_000 - fixed) // (4 * tn * states.shape[1])
        slots = min(slots, units, 1 + 2 * wide)
        if slots >= 2:
            return tn, slots
    return None


def fused(states, weights, token_ids, lengths, ratio_weight, wide, tn, slots):
    rows = states[0].shape[0] * wide // 4
    depth = states[0].shape[1]
    cols = weights[0].shape[1]
    units = 2 * cols // tn
    smem = pl.BlockSpec(memory_space=pltpu.SMEM)
    vmem = pl.BlockSpec(memory_space=pltpu.VMEM)
    hbm = pl.BlockSpec(memory_space=pl.ANY)
    out = jax.ShapeDtypeStruct((rows, cols), jnp.bfloat16)
    dma = pltpu.SemaphoreType.DMA
    pair = pl.pallas_call(
        functools.partial(kernel, wide, tn, slots),
        out_shape=(out, out),
        in_specs=[smem, smem] + [hbm] * 7,
        out_specs=(vmem, vmem),
        scratch_shapes=[
            pltpu.VMEM((2, wide, states[0].shape[0], depth), jnp.bfloat16),
            pltpu.VMEM((slots, 2, depth, tn), jnp.bfloat16),
            pltpu.VMEM((units, 2, 4, rows, tn), jnp.float32),
            pltpu.VMEM((units, 2, 2, rows, tn), jnp.bfloat16),
            pltpu.VMEM((units, 2, 2, rows, tn), jnp.bfloat16),
            pltpu.VMEM((units, 2, rows, tn), jnp.bfloat16),
            pltpu.VMEM((units, 2, rows, tn), jnp.bfloat16),
            pltpu.VMEM((units // 2, rows, tn), jnp.float32),
            pltpu.VMEM((rows, 1), jnp.float32),
            pltpu.VMEM((rows, 1), jnp.float32),
            pltpu.SMEM(ratio_weight.shape, jnp.float32),
            dma,
            dma((2,)),
            dma((2, 2, wide)),
            dma((2, wide)),
            dma((slots, 2)),
            dma((units,)),
            dma((units,)),
            dma((units,)),
            dma((units,)),
        ],
        compiler_params=pltpu.CompilerParams(
            collective_id=0, has_side_effects=True, vmem_limit_bytes=VMEM_BYTES
        ),
        name="rescore",
    )(token_ids, lengths, ratio_weight, *states, *weights)
    return pl.pallas_call(
        hand_over,
        out_shape=(out, out),
        in_specs=[hbm, hbm],
        out_specs=(hbm, hbm),
        scratch_shapes=[pltpu.VMEM((2, rows, cols), jnp.bfloat16), dma((2,)), dma((2,))],
        name="hand_over",
    )(*pair)


def local(
    wide,
    narrow,
    target_states,
    source_states,
    target_gate,
    target_up,
    source_gate,
    source_up,
    token_ids,
    lengths,
    ratio_weight,
):
    hidden_cols = target_gate.shape[1]
    own_rows = token_ids.shape[0]
    chosen = plan(target_states, target_gate, wide, narrow)
    if chosen is not None:
        return fused(
            (target_states, source_states),
            (target_gate, target_up, source_gate, source_up),
            token_ids,
            lengths,
            ratio_weight,
            wide,
            *chosen,
        )
    slot_count = own_rows // lengths.shape[0]
    slots = jnp.arange(slot_count, dtype=jnp.int32)
    live = (slots[None, :] < lengths[:, None]).reshape(-1).astype(jnp.float32)
    weight = ratio_weight[token_ids]
    target_terms = pair_project(
        target_gate, target_up, lax.all_gather(target_states, "wide", axis=0, tiled=True)
    )
    source_terms = pair_project(
        source_gate, source_up, lax.all_gather(source_states, "wide", axis=0, tiled=True)
    )
    target_sum, source_sum = (
        lax.psum_scatter(
            target_terms.astype(jnp.bfloat16), "narrow", scatter_dimension=0, tiled=True
        ).astype(jnp.float32),
        lax.psum_scatter(
            source_terms.astype(jnp.bfloat16), "narrow", scatter_dimension=0, tiled=True
        ).astype(jnp.float32),
    )
    target_act = gated(target_sum, hidden_cols)
    source_act = gated(source_sum, hidden_cols)
    target_out = (live[:, None] * target_act).astype(jnp.bfloat16)
    ratio_out = (live[:, None] * (target_act - weight[:, None] * source_act)).astype(jnp.bfloat16)
    return (target_out, ratio_out)


def solution(mesh):
    placed = (
        P(("groups", "wide"), "narrow"),
        P(("groups", "wide"), "narrow"),
        P("narrow", "wide"),
        P("narrow", "wide"),
        P("narrow", "wide"),
        P("narrow", "wide"),
        P(("groups", "narrow")),
        P(("groups", "narrow")),
        P(),
    )
    return jax.shard_map(
        functools.partial(local, mesh.shape["wide"], mesh.shape["narrow"]),
        mesh=mesh,
        in_specs=placed,
        out_specs=(P(("groups", "narrow"), "wide"), P(("groups", "narrow"), "wide")),
        check_vma=False,
    )
```
